128 devices in a mesh: fsdp: 8 (over y_lo, z), tensor: 16 (over x, y_hi, core).
Axes of the slice: x: 4, y: 4 (y_hi: 2, y_lo: 2; y = y_hi * 2 + y_lo), z: 4, core: 2. Of those that a mesh axis runs over, the one named last changes fastest.
Arguments:
- val_x: bfloat16 [4096, 8192], P('fsdp', 'tensor'), may hold values from -6 to 6
- val_cot: bfloat16 [4096, 16384], P('fsdp', 'tensor'), may hold values from -0.0010299683 to 0.0010299683
- second_moment: float32 [8192, 16384], P('fsdp', 'tensor'), may hold values from 0.01 to 1
- train_x: bfloat16 [2048, 8192], P('fsdp', 'tensor'), may hold values from -6 to 6
- train_cot: bfloat16 [2048, 16384], P('fsdp', 'tensor'), may hold values from -0.046875 to 0.046875
Outputs:
- scores: float32 [2048], P('fsdp')
The draws below stay inside these ranges and needn't reach their ends.
All inputs are finite; a program needn't handle non-finite values.
Results may differ from the reference program's by a relative error of at most 0.019.
Values may be sent and summed in bfloat16 or wider, within the bound.
No kernel may reach another device: no remote copies, remote signals or barrier semaphores. Data moves between devices by JAX's collectives and lax.ppermute only.
A program may use at most 128 MiB of HBM per device.

```python
import math
import jax
import jax.numpy as jnp
from jax import lax

D = 8192
FF = 16384
VT_DEV = 512
VTOKENS = 4096
TTOKENS = 2048
N_FSDP = 8


def spiked(entries, own_key, source, target, blocks, factor):
    def block_of(position):
        return (jnp.arange(entries.shape[position]) // (entries.shape[position] // blocks)).reshape((-1,) + (1,) * (entries.ndim - 1 - position))

    one_side = jax.random.permutation(own_key, blocks)[block_of(target)]
    far = (block_of(target) + blocks // 2) % blocks
    return jnp.where((block_of(source) == one_side) | (block_of(source) == far), factor * entries, entries)


def steps_of(rng, shape, cuts, least, largest):
    level = 1.0
    for position, parts in cuts:
        heights = jax.random.uniform(jax.random.fold_in(jax.random.fold_in(rng, 6), position), (parts,), jnp.float32, least / len(cuts), largest / len(cuts))
        level = level * jnp.repeat(jnp.exp(heights), shape[position] // parts).reshape((-1,) + (1,) * (len(shape) - 1 - position))
    return level


def scatter_about(rng, extent, width, bound, cuts=(), kind=jnp.bfloat16):
    drawn = width * jax.random.normal(rng, extent, jnp.float32)
    if cuts:
        drawn = drawn * steps_of(rng, extent, cuts, -0.22, 0.18)
    return jnp.clip(drawn, -bound, bound).astype(kind)


def noise_with(rng, dims, width, bound, pieces, heavy, held_as=jnp.bfloat16):
    result = width * jax.random.normal(rng, dims, jnp.float32)
    if pieces:
        result = result * steps_of(rng, dims, pieces, -0.22, 0.18)
    return jnp.clip(spiked(result, jax.random.fold_in(rng, 3), *heavy), -bound, bound).astype(held_as)


def setup_inputs(seed: int = 0) -> dict:
    seeds = jax.random.split(jax.random.key(seed), 6)
    val_x = noise_with(seeds[0], (VTOKENS, D), 1.0, 6.0, ((0, 8), (1, 16)), (0, 1, 16, 2.0))
    val_cot = scatter_about(seeds[1], (VTOKENS, FF), (1.0 / (VTOKENS * D) ** 0.5), 0.0010299683, ((0, 8), (1, 16)))
    second_moment = jnp.clip(jnp.exp(math.log(1.0) - 4.6051702 * jax.random.uniform(seeds[2], (D, FF), jnp.float32) ** steps_of(seeds[2], (D, FF), ((0, 8), (1, 16)), -0.2, 0.2)), 0.01, 1.0)
    train_x = scatter_about(seeds[3], (TTOKENS, D), 1.0, 6.0, ((0, 8), (1, 16)))
    train_cot = scatter_about(seeds[4], (TTOKENS, FF), FF ** -0.5, 0.046875, ((0, 8), (1, 16)))
    return dict(val_x=val_x, val_cot=val_cot, second_moment=second_moment, train_x=train_x, train_cot=train_cot)


EPSILON = 1e-08

def reference(val_x, val_cot, second_moment, train_x, train_cot):
    groups_x = val_x.reshape(N_FSDP, VT_DEV, D)
    groups_c = val_cot.reshape(N_FSDP, VT_DEV, FF)

    def add_group(total, pair):
        part = lax.dot_general(pair[0], pair[1], (((0,), (0,)), ((), ())), preferred_element_type=jnp.float32)
        part = lax.optimization_barrier(part.astype(jnp.bfloat16))
        return (total + part.astype(jnp.float32), None)
    grad, _ = lax.scan(add_group, jnp.zeros((D, FF), jnp.float32), (groups_x, groups_c))
    delta = (grad / (jnp.sqrt(second_moment) + EPSILON)).astype(jnp.bfloat16)
    shifted = jnp.dot(train_x, delta, preferred_element_type=jnp.float32)
    return lax.optimization_barrier(jnp.sum(shifted * train_cot.astype(jnp.float32), axis=1))
```

```python
import jax
import jax.numpy as jnp
import numpy as np
from jax import lax
from jax.experimental import pallas as pl
from jax.experimental.pallas import tpu as pltpu
from jax.sharding import PartitionSpec as P

EPSILON = 1e-08
BOTH = ("fsdp", "tensor")
F32 = jnp.float32

SIZES = {"yl": 2, "z": 4, "x": 4, "yh": 2, "core": 2}

TURN = (
    (4, 0, 6, 2, 1, 5, 3, 7),
    (5, 3, 7, 1, 6, 4, 2, 0),
    (2, 1, 0, 6, 5, 4, 7, 3),
    (1, 7, 5, 3, 0, 2, 4, 6),
    (1, 7, 2, 5, 4, 3, 0, 6),
    (6, 2, 0, 4, 1, 3, 7, 5),
    (7, 5, 4, 1, 3, 0, 6, 2),
    (0, 4, 6, 2, 7, 1, 5, 3),
)


def place_of(index):
    place = {}
    for name in reversed(SIZES):
        index, place[name] = divmod(index, SIZES[name])
    return place


def index_of(place):
    index = 0
    for name, size in SIZES.items():
        index = index * size + place[name] % size
    return index


def pairs_of(move):
    return [(i, index_of({**place_of(i), **move(place_of(i))})) for i in range(128)]


def turned(place):
    column, row = place["x"] * 2 + place["yh"], place["yl"] * 4 + place["z"]
    to = TURN[column][row]
    return {"yl": column // 4, "z": column % 4, "x": to // 2, "yh": to % 2}


def turn(array):
    return lax.ppermute(array, BOTH, pairs_of(turned))


def shift(array, name, by):
    return lax.ppermute(array, BOTH, pairs_of(lambda place: {name: place[name] + by}))


OFFSETS = ((0, 0), (0, -1), (0, 1), (0, 2), (1, 0), (1, -1), (1, 1), (1, 2))


def gathered(own, ring, half, last_by_half):
    ahead = shift(own, ring, 1)
    behind = shift(own, ring, -1)
    across = shift(own, ring, 2)
    other = shift(own, half, 1)
    other_ahead = shift(other, ring, 1)
    other_behind = shift(other, ring, -1)
    if last_by_half:
        other_across = shift(across, half, 1)
    else:
        other_across = shift(other, ring, 2)
    return [own, ahead, behind, across, other, other_ahead, other_behind, other_across]


def table():
    rows = []
    for i in range(128):
        place = place_of(i)
        row = place["yl"] * 4 + place["z"]
        cot_groups = [((place["yl"] + h) % 2) * 4 + (place["z"] + r) % 4 for h, r in OFFSETS]
        feature_groups = [
            TURN[row].index(((place["x"] + r) % 4) * 2 + (place["yh"] + h) % 2) for h, r in OFFSETS
        ]
        meets = [cot_groups.index(g) for g in feature_groups]
        rows.append(meets + feature_groups + [place["core"]])
    return np.array(rows, np.int32)


def fetch(sources, slots, sems):
    for k, source in enumerate(sources):
        pltpu.make_async_copy(source, slots.at[k], sems.at[k]).start()


def arrive(sources, slots, sems, k):
    pltpu.make_async_copy(sources[0], slots.at[k], sems.at[k]).wait()


def delta_kernel(*refs):
    where, refs = refs[0], refs[1:]
    cots, mine, theirs, moment = refs[:8], refs[8:16], refs[16:24], refs[24]
    out, c_slots, m_slots, t_slots, total, moments = refs[25:31]
    c_sems, m_sems, t_sems, sem = refs[31:]
    fetch(cots, c_slots, c_sems)
    fetch(mine, m_slots, m_sems)
    fetch(theirs, t_slots, t_sems)
    whole = pltpu.make_async_copy(moment, moments, sem)
    whole.start()
    for k in range(8):
        arrive(cots, c_slots, c_sems, k)
    total[...] = jnp.zeros_like(total)

    @pl.loop(0, 8)
    def _(k):
        arrive(mine, m_slots, m_sems, k)
        arrive(theirs, t_slots, t_sems, k)
        cot = c_slots[where[k]]
        for at, slots in ((0, m_slots), (512, t_slots)):
            total[at : at + 512, :] += lax.dot_general(
                slots[k], cot, (((0,), (0,)), ((), ())), preferred_element_type=F32
            )

    whole.wait()

    @pl.loop(0, 32)
    def _(r):
        at = pl.multiple_of(r * 32, 32)
        source = pl.multiple_of(jnp.where(where[16] == 0, at, (at + 512) % 1024), 32)
        scale = jnp.sqrt(moments[pl.ds(source, 32), :]) + EPSILON
        out[pl.ds(at, 32), :] = (total[pl.ds(at, 32), :] / scale).astype(jnp.bfloat16)


def score_kernel(*refs):
    where, delta, refs = refs[0], refs[1], refs[2:]
    cots, mine, theirs, out = refs[:8], refs[8:16], refs[16:24], refs[24]
    c_slots, m_slots, t_slots, c_sems, m_sems, t_sems = refs[25:]
    fetch(cots, c_slots, c_sems)
    fetch(mine, m_slots, m_sems)
    fetch(theirs, t_slots, t_sems)
    for k in range(8):
        arrive(cots, c_slots, c_sems, k)

    @pl.loop(0, 8)
    def _(k):
        arrive(mine, m_slots, m_sems, k)
        arrive(theirs, t_slots, t_sems, k)
        shifted = jnp.dot(m_slots[k], delta[:512, :], preferred_element_type=F32)
        shifted += jnp.dot(t_slots[k], delta[512:, :], preferred_element_type=F32)
        terms = shifted * c_slots[where[k]].astype(F32)
        part = terms[:, :128]
        for lanes in range(128, 1024, 128):
            part += terms[:, lanes : lanes + 128]
        out[where[8 + k]] = jnp.sum(part.T, axis=0, keepdims=True)


SMEM = pl.BlockSpec(memory_space=pltpu.SMEM)
VMEM = pl.BlockSpec(memory_space=pltpu.VMEM)
ANY = pl.BlockSpec(memory_space=pl.ANY)


def slots_of(blocks):
    return pltpu.VMEM((8, *blocks[0].shape), blocks[0].dtype)


def delta_of(where, cots, mine, theirs, moment):
    dma = pltpu.SemaphoreType.DMA
    return pl.pallas_call(
        delta_kernel,
        out_shape=jax.ShapeDtypeStruct((1024, 1024), jnp.bfloat16),
        in_specs=[SMEM] + [ANY] * 25,
        out_specs=VMEM,
        scratch_shapes=[
            slots_of(cots),
            slots_of(mine),
            slots_of(theirs),
            pltpu.VMEM((1024, 1024), F32),
            pltpu.VMEM((1024, 1024), F32),
            dma((8,)),
            dma((8,)),
            dma((8,)),
            dma,
        ],
        compiler_params=pltpu.CompilerParams(vmem_limit_bytes=48 * 2**20),
        cost_estimate=pl.CostEstimate(flops=2**33, bytes_accessed=22 * 2**20, transcendentals=2**20),
        name="delta",
    )(where, *cots, *mine, *theirs, moment)


def scores_of(where, delta, cots, mine, theirs):
    dma = pltpu.SemaphoreType.DMA
    return pl.pallas_call(
        score_kernel,
        out_shape=jax.ShapeDtypeStruct((8, 1, 256), F32),
        in_specs=[SMEM, VMEM] + [ANY] * 24,
        out_specs=VMEM,
        scratch_shapes=[slots_of(cots), slots_of(mine), slots_of(theirs), dma((8,)), dma((8,)), dma((8,))],
        compiler_params=pltpu.CompilerParams(vmem_limit_bytes=32 * 2**20),
        cost_estimate=pl.CostEstimate(flops=2**32, bytes_accessed=10 * 2**20, transcendentals=0),
        name="scores",
    )(where, delta, *cots, *mine, *theirs)


def per_device(val_x, val_cot, second_moment, train_x, train_cot):
    me = lax.axis_index("fsdp") * 16 + lax.axis_index("tensor")
    where = lax.dynamic_index_in_dim(jnp.asarray(table()), me, 0, keepdims=False)

    val_cots = gathered(val_cot, "z", "yl", True)
    val_mine = gathered(turn(val_x), "x", "yh", False)
    val_theirs = [shift(block, "core", 1) for block in val_mine]
    train_cots = gathered(train_cot, "z", "yl", True)
    train_mine = gathered(turn(train_x), "x", "yh", False)
    train_theirs = [shift(block, "core", 1) for block in train_mine]

    delta = delta_of(where, val_cots, val_mine, val_theirs, second_moment)
    block_scores = scores_of(where, delta, train_cots, train_mine, train_theirs)
    sent = jnp.broadcast_to(block_scores, (8, 16, 256)).reshape(128, 256)
    return jnp.sum(lax.all_to_all(sent, BOTH, 0, 0, tiled=True), axis=0)


def solution(mesh):
    placed = P("fsdp", "tensor")
    return jax.shard_map(
        per_device, mesh=mesh, in_specs=(placed,) * 5, out_specs=P("fsdp"), check_vma=False
    )
```

```python
import functools

import jax
import jax.numpy as jnp
import numpy as np
from jax import lax
from jax.experimental import pallas as pl
from jax.experimental.pallas import tpu as pltpu
from jax.sharding import PartitionSpec as P


EPSILON = 1e-08
BOTH = ("fsdp", "tensor")
F32 = jnp.float32

SIZES = {"yl": 2, "z": 4, "x": 4, "yh": 2, "core": 2}

TURN = (
    (
        (5, 4, 0, 6, 2, 3, 7, 1),
        (7, 1, 5, 4, 0, 3, 2, 6),
        (3, 2, 4, 0, 1, 5, 6, 7),
        (3, 2, 1, 7, 4, 5, 6, 0),
        (1, 7, 3, 2, 0, 6, 4, 5),
        (0, 6, 1, 2, 3, 7, 4, 5),
        (5, 3, 6, 1, 2, 4, 0, 7),
        (2, 1, 5, 4, 6, 3, 0, 7),
    ),
    (
        (0, 6, 2, 4, 7, 1, 5, 3),
        (5, 4, 7, 1, 2, 6, 0, 3),
        (6, 0, 1, 2, 4, 7, 3, 5),
        (1, 7, 3, 2, 6, 0, 4, 5),
        (3, 5, 7, 6, 4, 2, 1, 0),
        (4, 2, 3, 6, 1, 5, 7, 0),
        (7, 1, 5, 4, 6, 0, 2, 3),
        (7, 4, 6, 1, 5, 0, 2, 3),
    ),
)


def place_of(index):
    place = {}
    for name in reversed(SIZES):
        index, place[name] = divmod(index, SIZES[name])
    return place


def index_of(place):
    index = 0
    for name, size in SIZES.items():
        index = index * size + place[name] % size
    return index


def pairs_of(move):
    return [(i, index_of({**place_of(i), **move(place_of(i))})) for i in range(128)]


def turned(place):
    column, row = place["x"] * 2 + place["yh"], place["yl"] * 4 + place["z"]
    to = TURN[place["core"]][column][row]
    return {"yl": column // 4, "z": column % 4, "x": to // 2, "yh": to % 2}


def sent(array, move):
    return lax.ppermute(array, BOTH, pairs_of(move))


def way(place):
    return 1 - 2 * place["core"]


def fore(array, ring):
    return sent(array, lambda place: {ring: place[ring] + way(place)})


def aft(array, ring):
    return sent(array, lambda place: {ring: place[ring] - way(place)})


def across(array, axis):
    return sent(array, lambda place: {axis: place[axis] + 1})


OFFSETS = ((0, 0), (0, 1), (0, -1), (0, 2), (1, 0), (1, 1), (1, -1), (1, 2))


def gathered(own, ring, half, last_by_half):
    first = fore(own, ring)
    back = aft(own, ring)
    far = fore(first, ring)
    other = across(own, half)
    other_first = fore(other, ring)
    other_back = aft(other, ring)
    if last_by_half:
        other_far = across(far, half)
    else:
        other_far = fore(other_first, ring)
    return [own, first, back, far, other, other_first, other_back, other_far]


def swapped(blocks):
    return [across(block, "core") for block in blocks]


def cot_groups(place):
    return [
        ((place["yl"] + h) % 2) * 4 + (place["z"] - r * way(place)) % 4 for h, r in OFFSETS
    ]


def feature_groups(place):
    placed = TURN[place["core"]][place["yl"] * 4 + place["z"]]
    return [
        placed.index((place["x"] - r * way(place)) % 4 * 2 + (place["yh"] + h) % 2)
        for h, r in OFFSETS
    ]


def table():
    rows = []
    for i in range(128):
        place = place_of(i)
        partner = {**place, "core": 1 - place["core"]}
        groups, mine, theirs = cot_groups(place), feature_groups(place), feature_groups(partner)
        slots = [held.index(g) for held in (mine, theirs) for g in groups]
        rows.append(slots + groups + [place["core"]])
    return np.array(rows, np.int32)


def fetch(sources, slots, sems):
    for k, source in enumerate(sources):
        pltpu.make_async_copy(source, slots.at[k], sems.at[k]).start()


def arrive(slots, sems, k):
    pltpu.make_async_copy(slots.at[k], slots.at[k], sems.at[k]).wait()


def pass_on(where, slots, m_slots, t_slots, m_sems, t_sems, rest, sems):
    copies = []
    for j, slot in enumerate(slots):
        for side, (held, held_sems) in enumerate(((m_slots, m_sems), (t_slots, t_sems))):
            k = where[8 * side + slot]
            arrive(held, held_sems, k)
            copy = pltpu.make_async_copy(held.at[k], rest.at[j, side], sems.at[j, side])
            copy.start()
            copies.append(copy)
    return copies


MIB = (32, 32, 20, 12)


def early_delta_kernel(early, late, *refs):
    n = len(early)
    where, cots, mine, theirs = refs[0], refs[1 : 1 + n], refs[1 + n : 9 + n], refs[9 + n : 17 + n]
    total, rest, c_slots, m_slots, t_slots, c_sems, m_sems, t_sems, rest_sems = refs[17 + n :]
    fetch(cots, c_slots, c_sems)
    fetch(mine, m_slots, m_sems)
    fetch(theirs, t_slots, t_sems)
    for j, slot in enumerate(early):
        m, t = where[slot], where[8 + slot]
        arrive(c_slots, c_sems, j)
        arrive(m_slots, m_sems, m)
        arrive(t_slots, t_sems, t)
        for at, feature in ((0, m_slots[m]), (512, t_slots[t])):
            term = jnp.dot(feature, c_slots[j], preferred_element_type=F32)
            if j:
                total[at : at + 512, :] += term
            else:
                total[at : at + 512, :] = term
        if j == 2:
            copies = pass_on(where, late, m_slots, t_slots, m_sems, t_sems, rest, rest_sems)
    for copy in copies:
        copy.wait()


def late_delta_kernel(n, *refs):
    where, cots, moment, rest, partial = refs[0], refs[1 : 1 + n], *refs[1 + n : 4 + n]
    out, c_slots, total, moments, c_sems, sem = refs[4 + n :]
    fetch(cots, c_slots, c_sems)
    copy = pltpu.make_async_copy(moment, moments, sem)
    copy.start()
    for j in range(n):
        arrive(c_slots, c_sems, j)
        for side in range(2):
            term = jnp.dot(rest[j, side], c_slots[j], preferred_element_type=F32)
            so_far = total if j else partial
            at = 512 * side
            total[at : at + 512, :] = so_far[at : at + 512, :] + term
    copy.wait()

    @pl.loop(0, 32)
    def _(r):
        at = pl.multiple_of(r * 32, 32)
        source = pl.multiple_of(jnp.where(where[24] == 0, at, (at + 512) % 1024), 32)
        scale = jnp.sqrt(moments[pl.ds(source, 32), :]) + EPSILON
        out[pl.ds(at, 32), :] = (total[pl.ds(at, 32), :] / scale).astype(jnp.bfloat16)


def row_of(mine, theirs, delta, cot):
    shifted = jnp.dot(mine, delta[:512, :], preferred_element_type=F32)
    shifted += jnp.dot(theirs, delta[512:, :], preferred_element_type=F32)
    terms = shifted * cot.astype(F32)
    part = terms[:, :128]
    for lanes in range(128, 1024, 128):
        part += terms[:, lanes : lanes + 128]
    return jnp.sum(part.T, axis=0, keepdims=True)


def early_score_kernel(early, late, *refs):
    n = len(early)
    where, cots, mine, theirs = refs[0], refs[1 : 1 + n], refs[1 + n : 9 + n], refs[9 + n : 17 + n]
    delta, out, rest, c_slots, m_slots, t_slots, c_sems, m_sems, t_sems, rest_sems = refs[17 + n :]
    fetch(cots, c_slots, c_sems)
    fetch(mine, m_slots, m_sems)
    fetch(theirs, t_slots, t_sems)
    for j, slot in enumerate(early):
        m, t = where[slot], where[8 + slot]
        arrive(c_slots, c_sems, j)
        arrive(m_slots, m_sems, m)
        arrive(t_slots, t_sems, t)
        out[where[16 + slot]] = row_of(m_slots[m], t_slots[t], delta, c_slots[j])
        if j == 2:
            copies = pass_on(where, late, m_slots, t_slots, m_sems, t_sems, rest, rest_sems)
    for slot in late:
        out[where[16 + slot]] = jnp.zeros((1, 256), F32)
    for copy in copies:
        copy.wait()


def late_score_kernel(late, *refs):
    n = len(late)
    where, cots = refs[0], refs[1 : 1 + n]
    delta, rows, rest, out, c_slots, c_sems = refs[1 + n :]
    fetch(cots, c_slots, c_sems)
    out[...] = rows[...]
    for j, slot in enumerate(late):
        arrive(c_slots, c_sems, j)
        out[where[16 + slot]] = row_of(rest[j, 0], rest[j, 1], delta, c_slots[j])


SMEM = pl.BlockSpec(memory_space=pltpu.SMEM)
VMEM = pl.BlockSpec(memory_space=pltpu.VMEM)
ANY = pl.BlockSpec(memory_space=pl.ANY)
DMA = pltpu.SemaphoreType.DMA


def slots_of(count, rows, columns=512):
    return pltpu.VMEM((count, rows, columns), jnp.bfloat16)


def called(kernel, outs, scratch, mib, flops, moved, where, loose, held):
    return pl.pallas_call(
        kernel,
        out_shape=outs,
        in_specs=[SMEM] + [ANY] * len(loose) + [VMEM] * len(held),
        out_specs=jax.tree.map(lambda _: VMEM, outs),
        scratch_shapes=scratch,
        compiler_params=pltpu.CompilerParams(vmem_limit_bytes=mib * 2**20),
        cost_estimate=pl.CostEstimate(flops=flops, bytes_accessed=moved, transcendentals=0),
    )(where, *loose, *held)


def delta_of(where, cots, mine, theirs, moment, early, late):
    e, n = len(early), len(late)
    square = jax.ShapeDtypeStruct((1024, 1024), F32)
    rest = jax.ShapeDtypeStruct((n, 2, 512, 512), jnp.bfloat16)
    partial, rest = called(
        functools.partial(early_delta_kernel, early, late),
        (square, rest),
        [slots_of(e, 512, 1024), slots_of(8, 512), slots_of(8, 512), DMA((e,)), DMA((8,)), DMA((8,)), DMA((n, 2))],
        MIB[0],
        2**30 * e,
        20 * 2**20,
        where,
        [*(cots[k] for k in early), *mine, *theirs],
        [],
    )
    return called(
        functools.partial(late_delta_kernel, n),
        jax.ShapeDtypeStruct((1024, 1024), jnp.bfloat16),
        [slots_of(n, 512, 1024), pltpu.VMEM((1024, 1024), F32), pltpu.VMEM((1024, 1024), F32), DMA((n,)), DMA],
        MIB[1],
        2**30 * n,
        16 * 2**20,
        where,
        [*(cots[k] for k in late), moment],
        [rest, partial],
    )


def scores_of(where, delta, cots, mine, theirs, early, late):
    e, n = len(early), len(late)
    rows = jax.ShapeDtypeStruct((8, 1, 256), F32)
    rest = jax.ShapeDtypeStruct((n, 2, 256, 512), jnp.bfloat16)
    found, rest = called(
        functools.partial(early_score_kernel, early, late),
        (rows, rest),
        [slots_of(e, 256, 1024), slots_of(8, 256), slots_of(8, 256), DMA((e,)), DMA((8,)), DMA((8,)), DMA((n, 2))],
        MIB[2],
        2**29 * e,
        10 * 2**20,
        where,
        [*(cots[k] for k in early), *mine, *theirs],
        [delta],
    )
    return called(
        functools.partial(late_score_kernel, late),
        rows,
        [slots_of(n, 256, 1024), DMA((n,))],
        MIB[3],
        2**29 * n,
        4 * 2**20,
        where,
        [cots[k] for k in late],
        [delta, found, rest],
    )


def per_device(val_x, val_cot, second_moment, train_x, train_cot):
    me = lax.axis_index("fsdp") * 16 + lax.axis_index("tensor")
    where = lax.dynamic_index_in_dim(jnp.asarray(table()), me, 0, keepdims=False)

    val_cots = gathered(val_cot, "z", "yl", True)
    train_cots = gathered(train_cot, "z", "yl", True)
    val_mine = gathered(sent(lax.optimization_barrier(val_x.T), turned), "x", "yh", False)
    train_mine = gathered(sent(train_x, turned), "x", "yh", False)
    val_theirs, train_theirs = swapped(val_mine), swapped(train_mine)
    delta = delta_of(where, val_cots, val_mine, val_theirs, second_moment, (0, 1, 2, 3, 4), (5, 6, 7))
    block_scores = scores_of(
        where, delta, train_cots, train_mine, train_theirs, (0, 1, 2, 4, 5, 6), (3, 7)
    )
    shares = jnp.broadcast_to(block_scores, (8, 16, 256)).reshape(128, 256)
    return jnp.sum(lax.all_to_all(shares, BOTH, 0, 0, tiled=True), axis=0)


def solution(mesh):
    placed = P("fsdp", "tensor")
    return jax.shard_map(
        per_device, mesh=mesh, in_specs=(placed,) * 5, out_specs=P("fsdp"), check_vma=False
    )
```

```python
import functools

import jax
import jax.numpy as jnp
import numpy as np
from jax import lax
from jax.experimental import pallas as pl
from jax.experimental.pallas import tpu as pltpu
from jax.sharding import PartitionSpec as P


EPSILON = 1e-08
BOTH = ("fsdp", "tensor")
F32 = jnp.float32

SIZES = {"yl": 2, "z": 4, "x": 4, "yh": 2, "core": 2}

TURN = (
    (
        (5, 4, 0, 6, 2, 3, 7, 1),
        (7, 1, 5, 4, 0, 3, 2, 6),
        (3, 2, 4, 0, 1, 5, 6, 7),
        (3, 2, 1, 7, 4, 5, 6, 0),
        (1, 7, 3, 2, 0, 6, 4, 5),
        (0, 6, 1, 2, 3, 7, 4, 5),
        (5, 3, 6, 1, 2, 4, 0, 7),
        (2, 1, 5, 4, 6, 3, 0, 7),
    ),
    (
        (0, 6, 2, 4, 7, 1, 5, 3),
        (5, 4, 7, 1, 2, 6, 0, 3),
        (6, 0, 1, 2, 4, 7, 3, 5),
        (1, 7, 3, 2, 6, 0, 4, 5),
        (3, 5, 7, 6, 4, 2, 1, 0),
        (4, 2, 3, 6, 1, 5, 7, 0),
        (7, 1, 5, 4, 6, 0, 2, 3),
        (7, 4, 6, 1, 5, 0, 2, 3),
    ),
)


def place_of(index):
    place = {}
    for name in reversed(SIZES):
        index, place[name] = divmod(index, SIZES[name])
    return place


def index_of(place):
    index = 0
    for name, size in SIZES.items():
        index = index * size + place[name] % size
    return index


def pairs_of(move):
    return [(i, index_of({**place_of(i), **move(place_of(i))})) for i in range(128)]


def turned(place):
    column, row = place["x"] * 2 + place["yh"], place["yl"] * 4 + place["z"]
    to = TURN[place["core"]][column][row]
    return {"yl": column // 4, "z": column % 4, "x": to // 2, "yh": to % 2}


def sent(array, move):
    return lax.ppermute(array, BOTH, pairs_of(move))


def way(place):
    return 1 - 2 * place["core"]


def fore(array, ring):
    return sent(array, lambda place: {ring: place[ring] + way(place)})


def aft(array, ring):
    return sent(array, lambda place: {ring: place[ring] - way(place)})


def across(array, axis):
    return sent(array, lambda place: {axis: place[axis] + 1})


OFFSETS = ((0, 0), (0, 1), (0, -1), (0, 2), (1, 0), (1, 1), (1, -1), (1, 2))
VAL_ORDER, VAL_EARLY = (0, 1, 2, 3, 4, 5, 6, 7), 5
TRAIN_ORDER, TRAIN_EARLY = (0, 1, 2, 3, 4, 5, 6, 7), 6


def gathered(own, ring, half, last_by_half):
    first = fore(own, ring)
    back = aft(own, ring)
    far = fore(first, ring)
    other = across(own, half)
    other_first = fore(other, ring)
    other_back = aft(other, ring)
    if last_by_half:
        other_far = across(far, half)
    else:
        other_far = fore(other_first, ring)
    return [own, first, back, far, other, other_first, other_back, other_far]


def swapped(blocks):
    return [across(block, "core") for block in blocks]


def cot_groups(place):
    return [
        ((place["yl"] + h) % 2) * 4 + (place["z"] - r * way(place)) % 4 for h, r in OFFSETS
    ]


def feature_groups(place):
    placed = TURN[place["core"]][place["yl"] * 4 + place["z"]]
    return [
        placed.index((place["x"] - r * way(place)) % 4 * 2 + (place["yh"] + h) % 2)
        for h, r in OFFSETS
    ]


def table(order):
    rows = []
    for i in range(128):
        place = place_of(i)
        partner = {**place, "core": 1 - place["core"]}
        groups = [cot_groups(place)[k] for k in order]
        slots = [groups.index(g) for held in (place, partner) for g in feature_groups(held)]
        rows.append(slots + groups + [place["core"]])
    return rows


def tables():
    return np.array([v + t for v, t in zip(table(VAL_ORDER), table(TRAIN_ORDER))], np.int32)


def fetch(copies):
    for copy in copies:
        copy.start()
    return copies


def arrive(copies):
    for copy in copies:
        copy.wait()


def fetch_rows(sources, slots, sems):
    rows = sources[0].shape[0]
    return fetch(
        [
            pltpu.make_async_copy(source, slots.at[pl.ds(k * rows, rows)], sems.at[k])
            for k, source in enumerate(sources)
        ]
    )


def fetch_val(where, sides, slots, sems):
    copies = []
    for side, sources in enumerate(sides):
        for k, source in enumerate(sources):
            at = pl.multiple_of(where[8 * side + k] * 512, 512)
            target = slots.at[side, :, pl.ds(at, 512)]
            copies.append(pltpu.make_async_copy(source, target, sems.at[side, k]))
    return fetch(copies)


def fetch_train(where, sides, slots, sems):
    copies = []
    for side, sources in enumerate(sides):
        for k, source in enumerate(sources):
            at = pl.multiple_of(where[8 * side + k] * 256, 256)
            target = slots.at[pl.ds(at, 256), pl.ds(512 * side, 512)]
            copies.append(pltpu.make_async_copy(source, target, sems.at[side, k]))
    return fetch(copies)


MIB = (20, 20, 14, 8)
HALVES = (slice(0, 512), slice(512, 1024))


def early_delta_kernel(n, *refs):
    where, cots, mine, theirs = refs[0], refs[1 : 1 + n], refs[1 + n : 9 + n], refs[9 + n : 17 + n]
    total, rest, c_slots, f_slots, c_sems, f_sems, sem = refs[17 + n :]
    features = fetch_val(where, (mine, theirs), f_slots, f_sems)
    copies = fetch_rows(cots, c_slots, c_sems)
    arrive(features)
    handed = fetch([pltpu.make_async_copy(f_slots.at[:, :, pl.ds(512 * n, 512 * (8 - n))], rest, sem)])
    arrive(copies)
    for side, at in enumerate(HALVES):
        total[at, :] = jnp.dot(f_slots[side, :, : 512 * n], c_slots[...], preferred_element_type=F32)
    arrive(handed)


def scale_kernel(where, moments, out):
    @pl.loop(0, 64)
    def _(r):
        at = pl.multiple_of(r * 16, 16)
        source = pl.multiple_of(jnp.where(where[24] == 0, at, (at + 512) % 1024), 16)
        out[pl.ds(at, 16), :] = 1.0 / (jnp.sqrt(moments[pl.ds(source, 16), :]) + EPSILON)


def late_delta_kernel(n, *refs):
    cots = refs[1 : 1 + n]
    rest, partial, scale, out, c_slots, c_sems = refs[1 + n :]
    arrive(fetch_rows(cots, c_slots, c_sems))
    for side, at in enumerate(HALVES):
        grad = jnp.dot(rest[side], c_slots[...], preferred_element_type=F32) + partial[at, :]
        out[at, :] = (grad * scale[at, :]).astype(jnp.bfloat16)


def row_of(features, delta, cot):
    terms = jnp.dot(features, delta[...], preferred_element_type=F32) * cot.astype(F32)
    part = terms[:, :128]
    for lanes in range(128, 1024, 128):
        part += terms[:, lanes : lanes + 128]
    return jnp.sum(part.T, axis=0, keepdims=True)


def early_score_kernel(n, *refs):
    where, cots, mine, theirs = refs[0], refs[1 : 1 + n], refs[1 + n : 9 + n], refs[9 + n : 17 + n]
    delta, out, rest, c_slots, f_slots, c_sems, f_sems, sem = refs[17 + n :]
    features = fetch_train(where, (mine, theirs), f_slots, f_sems)
    copies = fetch_rows(cots, c_slots, c_sems)
    arrive(features)
    handed = fetch([pltpu.make_async_copy(f_slots.at[pl.ds(256 * n, 256 * (8 - n))], rest, sem)])
    for slot in range(n):
        copies[slot].wait()
        at = slice(256 * slot, 256 * slot + 256)
        out[where[16 + slot]] = row_of(f_slots[at, :], delta, c_slots[at, :])
    for slot in range(n, 8):
        out[where[16 + slot]] = jnp.zeros((1, 256), F32)
    arrive(handed)


def late_score_kernel(n, *refs):
    where, cots = refs[0], refs[1 : 1 + n]
    delta, rows, rest, out, c_slots, c_sems = refs[1 + n :]
    copies = fetch_rows(cots, c_slots, c_sems)
    for g in range(8):
        out[16 * g : 16 * g + 16] = jnp.broadcast_to(rows[g : g + 1], (16, 1, 256))
    for j in range(n):
        copies[j].wait()
        at = slice(256 * j, 256 * j + 256)
        row = row_of(rest[at, :], delta, c_slots[at, :])
        out[pl.ds(16 * where[24 - n + j], 16)] = jnp.broadcast_to(row[None], (16, 1, 256))


SMEM = pl.BlockSpec(memory_space=pltpu.SMEM)
VMEM = pl.BlockSpec(memory_space=pltpu.VMEM)
HBM = pl.BlockSpec(memory_space=pltpu.HBM)
DMA = pltpu.SemaphoreType.DMA


def slots_of(count, rows, columns=1024):
    return pltpu.VMEM((count * rows, columns), jnp.bfloat16)


def called(kernel, outs, scratch, mib, flops, moved, where, loose, held):
    return pl.pallas_call(
        kernel,
        out_shape=outs,
        in_specs=[SMEM] + [HBM] * len(loose) + [VMEM] * len(held),
        out_specs=jax.tree.map(lambda _: VMEM, outs),
        scratch_shapes=scratch,
        compiler_params=pltpu.CompilerParams(vmem_limit_bytes=mib * 2**20),
        cost_estimate=pl.CostEstimate(flops=flops, bytes_accessed=moved, transcendentals=0),
    )(where, *loose, *held)


def scale_of(where, moment):
    square = jax.ShapeDtypeStruct((1024, 1024), F32)
    return called(scale_kernel, square, [], 20, 2**21, 2**23, where, [], [moment])


def delta_of(where, cots, mine, theirs, scale, early):
    n = early
    square = jax.ShapeDtypeStruct((1024, 1024), F32)
    rest = jax.ShapeDtypeStruct((2, 512, 512 * (8 - n)), jnp.bfloat16)
    partial, rest = called(
        functools.partial(early_delta_kernel, n),
        (square, rest),
        [slots_of(n, 512), pltpu.VMEM((2, 512, 4096), jnp.bfloat16), DMA((n,)), DMA((2, 8)), DMA],
        MIB[0],
        2**30 * n,
        20 * 2**20,
        where,
        [*cots[:n], *mine, *theirs],
        [],
    )
    return called(
        functools.partial(late_delta_kernel, 8 - n),
        jax.ShapeDtypeStruct((1024, 1024), jnp.bfloat16),
        [slots_of(8 - n, 512), DMA((8 - n,))],
        MIB[1],
        2**30 * (8 - n),
        16 * 2**20,
        where,
        cots[n:],
        [rest, partial, scale],
    )


def scores_of(where, delta, cots, mine, theirs, early):
    n = early
    rows = jax.ShapeDtypeStruct((8, 1, 256), F32)
    rest = jax.ShapeDtypeStruct((256 * (8 - n), 1024), jnp.bfloat16)
    found, rest = called(
        functools.partial(early_score_kernel, n),
        (rows, rest),
        [slots_of(n, 256), slots_of(8, 256), DMA((n,)), DMA((2, 8)), DMA],
        MIB[2],
        2**29 * n,
        10 * 2**20,
        where,
        [*cots[:n], *mine, *theirs],
        [delta],
    )
    return called(
        functools.partial(late_score_kernel, 8 - n),
        jax.ShapeDtypeStruct((128, 1, 256), F32),
        [slots_of(8 - n, 256), DMA((8 - n,))],
        MIB[3],
        2**29 * (8 - n),
        4 * 2**20,
        where,
        cots[n:],
        [delta, found, rest],
    )


def per_device(val_x, val_cot, second_moment, train_x, train_cot):
    me = lax.axis_index("fsdp") * 16 + lax.axis_index("tensor")
    where = lax.dynamic_index_in_dim(jnp.asarray(tables()), me, 0, keepdims=False)
    val_where, train_where = where[:25], where[25:]

    val_cots = gathered(val_cot, "z", "yl", True)
    train_cots = gathered(train_cot, "z", "yl", True)
    val_mine = gathered(sent(lax.optimization_barrier(val_x.T), turned), "x", "yh", False)
    train_mine = gathered(sent(train_x, turned), "x", "yh", False)
    val_theirs, train_theirs = swapped(val_mine), swapped(train_mine)
    scale = scale_of(val_where, second_moment)
    delta = delta_of(
        val_where, [val_cots[k] for k in VAL_ORDER], val_mine, val_theirs, scale, VAL_EARLY
    )
    shares = scores_of(train_where, delta, [train_cots[k] for k in TRAIN_ORDER], train_mine, train_theirs, TRAIN_EARLY)
    return jnp.sum(lax.all_to_all(shares, BOTH, 0, 0, tiled=True), axis=(0, 1))


def solution(mesh):
    placed = P("fsdp", "tensor")
    return jax.shard_map(
        per_device, mesh=mesh, in_specs=(placed,) * 5, out_specs=P("fsdp"), check_vma=False
    )
```

```python
import functools

import jax
import jax.numpy as jnp
import numpy as np
from jax import lax
from jax.experimental import pallas as pl
from jax.experimental.pallas import tpu as pltpu
from jax.sharding import PartitionSpec as P


EPSILON = 1e-08
BOTH = ("fsdp", "tensor")
F32 = jnp.float32

SIZES = {"yl": 2, "z": 4, "x": 4, "yh": 2, "core": 2}

TURN = (
    (
        (2, 4, 6, 0, 5, 1, 3, 7),
        (5, 1, 3, 7, 0, 6, 4, 2),
        (6, 2, 0, 4, 3, 7, 5, 1),
        (1, 5, 7, 3, 6, 2, 0, 4),
        (7, 1, 3, 5, 6, 0, 2, 4),
        (6, 0, 2, 4, 3, 1, 7, 5),
        (5, 7, 1, 3, 0, 6, 4, 2),
        (2, 4, 6, 0, 1, 7, 5, 3),
    ),
    (
        (0, 6, 4, 2, 7, 3, 1, 5),
        (7, 3, 1, 5, 2, 4, 6, 0),
        (4, 0, 2, 6, 1, 5, 7, 3),
        (3, 7, 5, 1, 4, 0, 2, 6),
        (3, 5, 7, 1, 4, 2, 0, 6),
        (4, 2, 0, 6, 7, 5, 3, 1),
        (1, 3, 5, 7, 2, 4, 6, 0),
        (0, 6, 4, 2, 5, 3, 1, 7),
    ),
)


def place_of(index):
    place = {}
    for name in reversed(SIZES):
        index, place[name] = divmod(index, SIZES[name])
    return place


def index_of(place):
    index = 0
    for name, size in SIZES.items():
        index = index * size + place[name] % size
    return index


def pairs_of(move):
    return [(i, index_of({**place_of(i), **move(place_of(i))})) for i in range(128)]


def turned(place):
    column, row = place["x"] * 2 + place["yh"], place["yl"] * 4 + place["z"]
    to = TURN[place["core"]][column][row]
    return {"yl": column // 4, "z": column % 4, "x": to // 2, "yh": to % 2}


def sent(array, move):
    return lax.ppermute(array, BOTH, pairs_of(move))


def way(place):
    return 1 - 2 * place["core"]


def fore(array, ring):
    return sent(array, lambda place: {ring: place[ring] + way(place)})


def aft(array, ring):
    return sent(array, lambda place: {ring: place[ring] - way(place)})


def across(array, axis):
    return sent(array, lambda place: {axis: place[axis] + 1})


OFFSETS = ((0, 0), (0, 1), (0, -1), (0, 2), (1, 0), (1, 1), (1, -1), (1, 2))
VAL_ORDER, VAL_EARLY = (0, 1, 2, 3, 4, 5, 6, 7), 5
TRAIN_ORDER, TRAIN_EARLY = (0, 1, 2, 3, 4, 5, 6, 7), 6


def gathered(own, ring, half, last_by_half):
    first = fore(own, ring)
    back = aft(own, ring)
    far = fore(first, ring)
    other = across(own, half)
    other_first = fore(other, ring)
    other_back = aft(other, ring)
    if last_by_half:
        other_far = across(far, half)
    else:
        other_far = fore(other_first, ring)
    return [own, first, back, far, other, other_first, other_back, other_far]


def swapped(blocks):
    return [across(block, "core") for block in blocks]


def cot_groups(place):
    return [
        ((place["yl"] + h) % 2) * 4 + (place["z"] - r * way(place)) % 4 for h, r in OFFSETS
    ]


def feature_groups(place):
    placed = TURN[place["core"]][place["yl"] * 4 + place["z"]]
    return [
        placed.index((place["x"] - r * way(place)) % 4 * 2 + (place["yh"] + h) % 2)
        for h, r in OFFSETS
    ]


def table(order):
    rows = []
    for i in range(128):
        place = place_of(i)
        partner = {**place, "core": 1 - place["core"]}
        groups = [cot_groups(place)[k] for k in order]
        slots = [groups.index(g) for held in (place, partner) for g in feature_groups(held)]
        rows.append(slots + groups + [place["core"]])
    return rows


def tables():
    return np.array([v + t for v, t in zip(table(VAL_ORDER), table(TRAIN_ORDER))], np.int32)


def fetch(copies):
    for copy in copies:
        copy.start()
    return copies


def arrive(copies):
    for copy in copies:
        copy.wait()


def fetch_rows(sources, slots, sems):
    rows = sources[0].shape[0]
    return fetch(
        [
            pltpu.make_async_copy(source, slots.at[pl.ds(k * rows, rows)], sems.at[k])
            for k, source in enumerate(sources)
        ]
    )


def fetch_val(where, sides, slots, sems):
    copies = []
    for side, sources in enumerate(sides):
        for k, source in enumerate(sources):
            at = pl.multiple_of(where[8 * side + k] * 512, 512)
            target = slots.at[side, :, pl.ds(at, 512)]
            copies.append(pltpu.make_async_copy(source, target, sems.at[side, k]))
    return fetch(copies)


def fetch_train(where, sides, slots, sems):
    copies = []
    for side, sources in enumerate(sides):
        for k, source in enumerate(sources):
            at = pl.multiple_of(where[8 * side + k] * 256, 256)
            target = slots.at[pl.ds(at, 256), pl.ds(512 * side, 512)]
            copies.append(pltpu.make_async_copy(source, target, sems.at[side, k]))
    return fetch(copies)


MIB = (20, 20, 14, 8)
HALVES = (slice(0, 512), slice(512, 1024))


def early_delta_kernel(n, *refs):
    where, cots, mine, theirs = refs[0], refs[1 : 1 + n], refs[1 + n : 9 + n], refs[9 + n : 17 + n]
    total, rest, c_slots, f_slots, c_sems, f_sems, sem = refs[17 + n :]
    features = fetch_val(where, (mine, theirs), f_slots, f_sems)
    copies = fetch_rows(cots, c_slots, c_sems)
    arrive(features)
    handed = fetch([pltpu.make_async_copy(f_slots.at[:, :, pl.ds(512 * n, 512 * (8 - n))], rest, sem)])
    arrive(copies)
    for side, at in enumerate(HALVES):
        total[at, :] = jnp.dot(f_slots[side, :, : 512 * n], c_slots[...], preferred_element_type=F32)
    arrive(handed)


def scale_kernel(where, moments, out):
    @pl.loop(0, 64)
    def _(r):
        at = pl.multiple_of(r * 16, 16)
        source = pl.multiple_of(jnp.where(where[24] == 0, at, (at + 512) % 1024), 16)
        out[pl.ds(at, 16), :] = 1.0 / (jnp.sqrt(moments[pl.ds(source, 16), :]) + EPSILON)


def late_delta_kernel(n, *refs):
    cots = refs[1 : 1 + n]
    rest, partial, scale, out, c_slots, c_sems = refs[1 + n :]
    arrive(fetch_rows(cots, c_slots, c_sems))
    for side, at in enumerate(HALVES):
        grad = jnp.dot(rest[side], c_slots[...], preferred_element_type=F32) + partial[at, :]
        out[at, :] = (grad * scale[at, :]).astype(jnp.bfloat16)


def row_of(features, delta, cot):
    terms = jnp.dot(features, delta[...], preferred_element_type=F32) * cot.astype(F32)
    part = terms[:, :128]
    for lanes in range(128, 1024, 128):
        part += terms[:, lanes : lanes + 128]
    return jnp.sum(part.T, axis=0, keepdims=True)


def early_score_kernel(n, *refs):
    where, cots, mine, theirs = refs[0], refs[1 : 1 + n], refs[1 + n : 9 + n], refs[9 + n : 17 + n]
    delta, out, rest, c_slots, f_slots, c_sems, f_sems, sem = refs[17 + n :]
    features = fetch_train(where, (mine, theirs), f_slots, f_sems)
    copies = fetch_rows(cots, c_slots, c_sems)
    arrive(features)
    handed = fetch([pltpu.make_async_copy(f_slots.at[pl.ds(256 * n, 256 * (8 - n))], rest, sem)])
    for slot in range(n):
        copies[slot].wait()
        at = slice(256 * slot, 256 * slot + 256)
        out[where[16 + slot]] = row_of(f_slots[at, :], delta, c_slots[at, :])
    for slot in range(n, 8):
        out[where[16 + slot]] = jnp.zeros((1, 256), F32)
    arrive(handed)


def late_score_kernel(n, *refs):
    where, cots = refs[0], refs[1 : 1 + n]
    delta, rows, rest, out, c_slots, c_sems = refs[1 + n :]
    copies = fetch_rows(cots, c_slots, c_sems)
    for g in range(8):
        out[16 * g : 16 * g + 16] = jnp.broadcast_to(rows[g : g + 1], (16, 1, 256))
    for j in range(n):
        copies[j].wait()
        at = slice(256 * j, 256 * j + 256)
        row = row_of(rest[at, :], delta, c_slots[at, :])
        out[pl.ds(16 * where[24 - n + j], 16)] = jnp.broadcast_to(row[None], (16, 1, 256))


SMEM = pl.BlockSpec(memory_space=pltpu.SMEM)
VMEM = pl.BlockSpec(memory_space=pltpu.VMEM)
HBM = pl.BlockSpec(memory_space=pltpu.HBM)
DMA = pltpu.SemaphoreType.DMA


def slots_of(count, rows, columns=1024):
    return pltpu.VMEM((count * rows, columns), jnp.bfloat16)


def called(kernel, outs, scratch, mib, flops, moved, where, loose, held):
    return pl.pallas_call(
        kernel,
        out_shape=outs,
        in_specs=[SMEM] + [HBM] * len(loose) + [VMEM] * len(held),
        out_specs=jax.tree.map(lambda _: VMEM, outs),
        scratch_shapes=scratch,
        compiler_params=pltpu.CompilerParams(vmem_limit_bytes=mib * 2**20),
        cost_estimate=pl.CostEstimate(flops=flops, bytes_accessed=moved, transcendentals=0),
    )(where, *loose, *held)


def scale_of(where, moment):
    square = jax.ShapeDtypeStruct((1024, 1024), F32)
    return called(scale_kernel, square, [], 20, 2**21, 2**23, where, [], [moment])


def delta_of(where, cots, mine, theirs, scale, early):
    n = early
    square = jax.ShapeDtypeStruct((1024, 1024), F32)
    rest = jax.ShapeDtypeStruct((2, 512, 512 * (8 - n)), jnp.bfloat16)
    partial, rest = called(
        functools.partial(early_delta_kernel, n),
        (square, rest),
        [slots_of(n, 512), pltpu.VMEM((2, 512, 4096), jnp.bfloat16), DMA((n,)), DMA((2, 8)), DMA],
        MIB[0],
        2**30 * n,
        20 * 2**20,
        where,
        [*cots[:n], *mine, *theirs],
        [],
    )
    return called(
        functools.partial(late_delta_kernel, 8 - n),
        jax.ShapeDtypeStruct((1024, 1024), jnp.bfloat16),
        [slots_of(8 - n, 512), DMA((8 - n,))],
        MIB[1],
        2**30 * (8 - n),
        16 * 2**20,
        where,
        cots[n:],
        [rest, partial, scale],
    )


def scores_of(where, delta, cots, mine, theirs, early):
    n = early
    rows = jax.ShapeDtypeStruct((8, 1, 256), F32)
    rest = jax.ShapeDtypeStruct((256 * (8 - n), 1024), jnp.bfloat16)
    found, rest = called(
        functools.partial(early_score_kernel, n),
        (rows, rest),
        [slots_of(n, 256), slots_of(8, 256), DMA((n,)), DMA((2, 8)), DMA],
        MIB[2],
        2**29 * n,
        10 * 2**20,
        where,
        [*cots[:n], *mine, *theirs],
        [delta],
    )
    return called(
        functools.partial(late_score_kernel, 8 - n),
        jax.ShapeDtypeStruct((128, 1, 256), F32),
        [slots_of(8 - n, 256), DMA((8 - n,))],
        MIB[3],
        2**29 * (8 - n),
        4 * 2**20,
        where,
        cots[n:],
        [delta, found, rest],
    )


def per_device(val_x, val_cot, second_moment, train_x, train_cot):
    me = lax.axis_index("fsdp") * 16 + lax.axis_index("tensor")
    where = lax.dynamic_index_in_dim(jnp.asarray(tables()), me, 0, keepdims=False)
    val_where, train_where = where[:25], where[25:]

    val_cots = gathered(val_cot, "z", "yl", True)
    train_cots = gathered(train_cot, "z", "yl", True)
    val_mine = gathered(sent(lax.optimization_barrier(val_x.T), turned), "x", "yh", False)
    train_mine = gathered(sent(train_x, turned), "x", "yh", False)
    val_theirs, train_theirs = swapped(val_mine), swapped(train_mine)
    scale = scale_of(val_where, second_moment)
    delta = delta_of(
        val_where, [val_cots[k] for k in VAL_ORDER], val_mine, val_theirs, scale, VAL_EARLY
    )
    shares = scores_of(train_where, delta, [train_cots[k] for k in TRAIN_ORDER], train_mine, train_theirs, TRAIN_EARLY)
    return jnp.sum(lax.all_to_all(shares, BOTH, 0, 0, tiled=True), axis=(0, 1))


def solution(mesh):
    placed = P("fsdp", "tensor")
    return jax.shard_map(
        per_device, mesh=mesh, in_specs=(placed,) * 5, out_specs=P("fsdp"), check_vma=False
    )
```

```python
import functools

import jax
import jax.numpy as jnp
import numpy as np
from jax import lax
from jax.experimental import pallas as pl
from jax.experimental.pallas import tpu as pltpu
from jax.sharding import PartitionSpec as P


EPSILON = 1e-08
BOTH = ("fsdp", "tensor")
F32 = jnp.float32

SIZES = {"yl": 2, "z": 4, "x": 4, "yh": 2, "core": 2}

TURN = (
    (
        (2, 4, 6, 0, 5, 1, 3, 7),
        (5, 1, 3, 7, 0, 6, 4, 2),
        (6, 2, 0, 4, 3, 7, 5, 1),
        (1, 5, 7, 3, 6, 2, 0, 4),
        (7, 1, 3, 5, 6, 0, 2, 4),
        (6, 0, 2, 4, 3, 1, 7, 5),
        (5, 7, 1, 3, 0, 6, 4, 2),
        (2, 4, 6, 0, 1, 7, 5, 3),
    ),
    (
        (0, 6, 4, 2, 7, 3, 1, 5),
        (7, 3, 1, 5, 2, 4, 6, 0),
        (4, 0, 2, 6, 1, 5, 7, 3),
        (3, 7, 5, 1, 4, 0, 2, 6),
        (3, 5, 7, 1, 4, 2, 0, 6),
        (4, 2, 0, 6, 7, 5, 3, 1),
        (1, 3, 5, 7, 2, 4, 6, 0),
        (0, 6, 4, 2, 5, 3, 1, 7),
    ),
)


def place_of(index):
    place = {}
    for name in reversed(SIZES):
        index, place[name] = divmod(index, SIZES[name])
    return place


def index_of(place):
    index = 0
    for name, size in SIZES.items():
        index = index * size + place[name] % size
    return index


def pairs_of(move):
    return [(i, index_of({**place_of(i), **move(place_of(i))})) for i in range(128)]


def turned(place):
    column, row = place["x"] * 2 + place["yh"], place["yl"] * 4 + place["z"]
    to = TURN[place["core"]][column][row]
    return {"yl": column // 4, "z": column % 4, "x": to // 2, "yh": to % 2}


def sent(array, move):
    return lax.ppermute(array, BOTH, pairs_of(move))


def way(place):
    return 1 - 2 * place["core"]


def fore(array, ring):
    return sent(array, lambda place: {ring: place[ring] + way(place)})


def aft(array, ring):
    return sent(array, lambda place: {ring: place[ring] - way(place)})


def across(array, axis):
    return sent(array, lambda place: {axis: place[axis] + 1})


OFFSETS = ((0, 0), (0, 1), (0, -1), (0, 2), (1, 0), (1, 1), (1, -1), (1, 2))
VAL_ORDER, VAL_EARLY = (0, 1, 2, 3, 4, 5, 6, 7), 5
TRAIN_ORDER, TRAIN_EARLY = (0, 1, 2, 3, 4, 5, 6, 7), 6


def gathered(own, ring, half, last_by_half):
    first = fore(own, ring)
    back = aft(own, ring)
    far = fore(first, ring)
    other = across(own, half)
    other_first = fore(other, ring)
    other_back = aft(other, ring)
    if last_by_half:
        other_far = across(far, half)
    else:
        other_far = fore(other_first, ring)
    return [own, first, back, far, other, other_first, other_back, other_far]


def swapped(blocks):
    return [across(block, "core") for block in blocks]


def cot_groups(place):
    return [
        ((place["yl"] + h) % 2) * 4 + (place["z"] - r * way(place)) % 4 for h, r in OFFSETS
    ]


def feature_groups(place):
    placed = TURN[place["core"]][place["yl"] * 4 + place["z"]]
    return [
        placed.index((place["x"] - r * way(place)) % 4 * 2 + (place["yh"] + h) % 2)
        for h, r in OFFSETS
    ]


def table(order):
    rows = []
    for i in range(128):
        place = place_of(i)
        partner = {**place, "core": 1 - place["core"]}
        groups = [cot_groups(place)[k] for k in order]
        slots = [groups.index(g) for held in (place, partner) for g in feature_groups(held)]
        rows.append(slots + groups + [place["core"]])
    return rows


def tables():
    return np.array([v + t for v, t in zip(table(VAL_ORDER), table(TRAIN_ORDER))], np.int32)


def fetch(copies):
    for copy in copies:
        copy.start()
    return copies


def arrive(copies):
    for copy in copies:
        copy.wait()


def fetch_rows(sources, slots, sems):
    rows = sources[0].shape[0]
    return fetch(
        [
            pltpu.make_async_copy(source, slots.at[pl.ds(k * rows, rows)], sems.at[k])
            for k, source in enumerate(sources)
        ]
    )


def fetch_val(where, sides, slots, sems):
    copies = []
    for side, sources in enumerate(sides):
        for k, source in enumerate(sources):
            at = pl.multiple_of(where[8 * side + k] * 512, 512)
            target = slots.at[side, :, pl.ds(at, 512)]
            copies.append(pltpu.make_async_copy(source, target, sems.at[side, k]))
    return fetch(copies)


def fetch_train(where, sides, slots, sems):
    copies = []
    for side, sources in enumerate(sides):
        for k, source in enumerate(sources):
            at = pl.multiple_of(where[8 * side + k] * 256, 256)
            target = slots.at[pl.ds(at, 256), pl.ds(512 * side, 512)]
            copies.append(pltpu.make_async_copy(source, target, sems.at[side, k]))
    return fetch(copies)


MIB = (20, 20, 14, 8)
HALVES = (slice(0, 512), slice(512, 1024))


def early_delta_kernel(n, *refs):
    where, cots, mine, theirs = refs[0], refs[1 : 1 + n], refs[1 + n : 9 + n], refs[9 + n : 17 + n]
    total, rest, c_slots, f_slots, c_sems, f_sems, sem = refs[17 + n :]
    features = fetch_val(where, (mine, theirs), f_slots, f_sems)
    copies = fetch_rows(cots, c_slots, c_sems)
    arrive(features)
    handed = fetch([pltpu.make_async_copy(f_slots.at[:, :, pl.ds(512 * n, 512 * (8 - n))], rest, sem)])
    arrive(copies)
    for side, at in enumerate(HALVES):
        total[at, :] = jnp.dot(f_slots[side, :, : 512 * n], c_slots[...], preferred_element_type=F32)
    arrive(handed)


def scale_kernel(where, moment, out):
    out[...] = 1.0 / (jnp.sqrt(moment[...]) + EPSILON)


def late_delta_kernel(n, *refs):
    cots = refs[1 : 1 + n]
    rest, partial, scale, out, c_slots, c_sems = refs[1 + n :]
    arrive(fetch_rows(cots, c_slots, c_sems))
    for side, at in enumerate(HALVES):
        grad = jnp.dot(rest[side], c_slots[...], preferred_element_type=F32) + partial[at, :]
        out[at, :] = (grad * scale[at, :]).astype(jnp.bfloat16)


def row_of(features, delta, cot):
    terms = jnp.dot(features, delta[...], preferred_element_type=F32) * cot.astype(F32)
    part = terms[:, :128]
    for lanes in range(128, 1024, 128):
        part += terms[:, lanes : lanes + 128]
    return jnp.sum(part.T, axis=0, keepdims=True)


def early_score_kernel(n, *refs):
    where, cots, mine, theirs = refs[0], refs[1 : 1 + n], refs[1 + n : 9 + n], refs[9 + n : 17 + n]
    delta, out, rest, c_slots, f_slots, c_sems, f_sems, sem = refs[17 + n :]
    features = fetch_train(where, (mine, theirs), f_slots, f_sems)
    copies = fetch_rows(cots, c_slots, c_sems)
    arrive(features)
    handed = fetch([pltpu.make_async_copy(f_slots.at[pl.ds(256 * n, 256 * (8 - n))], rest, sem)])
    for slot in range(n):
        copies[slot].wait()
        at = slice(256 * slot, 256 * slot + 256)
        out[where[16 + slot]] = row_of(f_slots[at, :], delta, c_slots[at, :])
    for slot in range(n, 8):
        out[where[16 + slot]] = jnp.zeros((1, 256), F32)
    arrive(handed)


def late_score_kernel(n, *refs):
    where, cots = refs[0], refs[1 : 1 + n]
    delta, rows, rest, out, c_slots, c_sems = refs[1 + n :]
    copies = fetch_rows(cots, c_slots, c_sems)
    for g in range(8):
        out[16 * g : 16 * g + 16] = jnp.broadcast_to(rows[g : g + 1], (16, 1, 256))
    for j in range(n):
        copies[j].wait()
        at = slice(256 * j, 256 * j + 256)
        row = row_of(rest[at, :], delta, c_slots[at, :])
        out[pl.ds(16 * where[24 - n + j], 16)] = jnp.broadcast_to(row[None], (16, 1, 256))


SMEM = pl.BlockSpec(memory_space=pltpu.SMEM)
VMEM = pl.BlockSpec(memory_space=pltpu.VMEM)
HBM = pl.BlockSpec(memory_space=pltpu.HBM)
DMA = pltpu.SemaphoreType.DMA


def slots_of(count, rows, columns=1024):
    return pltpu.VMEM((count * rows, columns), jnp.bfloat16)


def called(kernel, outs, scratch, mib, flops, moved, where, loose, held):
    return pl.pallas_call(
        kernel,
        out_shape=outs,
        in_specs=[SMEM] + [HBM] * len(loose) + [VMEM] * len(held),
        out_specs=jax.tree.map(lambda _: VMEM, outs),
        scratch_shapes=scratch,
        compiler_params=pltpu.CompilerParams(vmem_limit_bytes=mib * 2**20),
        cost_estimate=pl.CostEstimate(flops=flops, bytes_accessed=moved, transcendentals=0),
    )(where, *loose, *held)


def scale_of(where, moment):
    return pl.pallas_call(
        scale_kernel,
        out_shape=jax.ShapeDtypeStruct((1024, 1024), F32),
        grid_spec=pltpu.PrefetchScalarGridSpec(
            num_scalar_prefetch=1,
            grid=(4,),
            in_specs=[pl.BlockSpec((256, 1024), lambda r, where: ((r + 2 * where[24]) % 4, 0))],
            out_specs=pl.BlockSpec((256, 1024), lambda r, where: (r, 0)),
        ),
        compiler_params=pltpu.CompilerParams(vmem_limit_bytes=8 * 2**20),
        cost_estimate=pl.CostEstimate(flops=2**21, bytes_accessed=2**23, transcendentals=0),
        name="get_scale",
    )(where, moment)


def delta_of(where, cots, mine, theirs, scale, early):
    n = early
    square = jax.ShapeDtypeStruct((1024, 1024), F32)
    rest = jax.ShapeDtypeStruct((2, 512, 512 * (8 - n)), jnp.bfloat16)
    partial, rest = called(
        functools.partial(early_delta_kernel, n),
        (square, rest),
        [slots_of(n, 512), pltpu.VMEM((2, 512, 4096), jnp.bfloat16), DMA((n,)), DMA((2, 8)), DMA],
        MIB[0],
        2**30 * n,
        20 * 2**20,
        where,
        [*cots[:n], *mine, *theirs],
        [],
    )
    return called(
        functools.partial(late_delta_kernel, 8 - n),
        jax.ShapeDtypeStruct((1024, 1024), jnp.bfloat16),
        [slots_of(8 - n, 512), DMA((8 - n,))],
        MIB[1],
        2**30 * (8 - n),
        16 * 2**20,
        where,
        cots[n:],
        [rest, partial, scale],
    )


def scores_of(where, delta, cots, mine, theirs, early):
    n = early
    rows = jax.ShapeDtypeStruct((8, 1, 256), F32)
    rest = jax.ShapeDtypeStruct((256 * (8 - n), 1024), jnp.bfloat16)
    found, rest = called(
        functools.partial(early_score_kernel, n),
        (rows, rest),
        [slots_of(n, 256), slots_of(8, 256), DMA((n,)), DMA((2, 8)), DMA],
        MIB[2],
        2**29 * n,
        10 * 2**20,
        where,
        [*cots[:n], *mine, *theirs],
        [delta],
    )
    return called(
        functools.partial(late_score_kernel, 8 - n),
        jax.ShapeDtypeStruct((128, 1, 256), F32),
        [slots_of(8 - n, 256), DMA((8 - n,))],
        MIB[3],
        2**29 * (8 - n),
        4 * 2**20,
        where,
        cots[n:],
        [delta, found, rest],
    )


def per_device(val_x, val_cot, second_moment, train_x, train_cot):
    me = lax.axis_index("fsdp") * 16 + lax.axis_index("tensor")
    where = lax.dynamic_index_in_dim(jnp.asarray(tables()), me, 0, keepdims=False)
    val_where, train_where = where[:25], where[25:]

    val_cots = gathered(val_cot, "z", "yl", True)
    train_cots = gathered(train_cot, "z", "yl", True)
    val_mine = gathered(sent(lax.optimization_barrier(val_x.T), turned), "x", "yh", False)
    train_mine = gathered(sent(train_x, turned), "x", "yh", False)
    val_theirs, train_theirs = swapped(val_mine), swapped(train_mine)
    scale = scale_of(val_where, second_moment)
    delta = delta_of(
        val_where, [val_cots[k] for k in VAL_ORDER], val_mine, val_theirs, scale, VAL_EARLY
    )
    shares = scores_of(train_where, delta, [train_cots[k] for k in TRAIN_ORDER], train_mine, train_theirs, TRAIN_EARLY)
    return jnp.sum(lax.all_to_all(shares, BOTH, 0, 0, tiled=True), axis=(0, 1))


def solution(mesh):
    placed = P("fsdp", "tensor")
    return jax.shard_map(
        per_device, mesh=mesh, in_specs=(placed,) * 5, out_specs=P("fsdp"), check_vma=False
    )
```
